1024 devices in a mesh: pole: 8 (over x), row: 16 (over y, z_lo), col: 8 (over z_hi, core).
Axes of the slice: x: 8, y: 8, z: 8 (z_hi: 4, z_lo: 2; z = z_hi * 2 + z_lo), core: 2. Of those that a mesh axis runs over, the one named last changes fastest.
Arguments:
- factor: float32 [8, 2, 512, 16, 128], P('pole', None, 'row'), may hold values from -0.375 to 0.375
- green: float32 [8, 2, 512, 512], P('pole', None, 'row', 'col'), may hold values from -6 to 6
- diag_inv: float32 [8, 2, 16, 128, 128], P('pole', None, 'row'), may hold values from -6 to 6
- pole_weight: float32 [8, 2], P('pole'), may hold values from -4 to 4
- structure: int32 [16, 8], replicated, may hold values 0 or 1
- widths: int32 [16], replicated, may hold values from 32 to 128, as said below
Outputs:
- density_off: float32 [16, 128, 512], P('row', None, 'col')
- density_diag: float32 [16, 128, 128], P('row')
The draws below stay inside these ranges and needn't reach their ends.
Inputs may be any that keep to these rules, and one draw needn't show every extreme that they name: `widths`: some supernode has all 128 columns.
All inputs are finite; a program needn't handle non-finite values.
Results may differ from the reference program's by a relative error of at most 0.0001.
Values sent between devices are 32-bit elements; how exact they have to be, the bound alone decides.
No kernel may reach another device: no remote copies, remote signals or barrier semaphores. Data moves between devices by JAX's collectives and lax.ppermute only.
A program may use at most 32 MiB of HBM per device.

```python
import jax
import jax.numpy as jnp
from jax import lax

W = 128
NA = 512
NB = 8
S = 16
POLES = 8


def draw_widths(key, part):
    first_key = jax.random.fold_in(key, 11)
    second_key = jax.random.fold_in(key, 12)
    values = jax.random.randint(first_key, (S,), W // 4, W + 1)
    place = jax.random.randint(second_key, (), 0, S)
    return jnp.where(jnp.arange(S) == place, W, values).astype(jnp.int32)


def set_ends(values, own_key, smallest, top_value):
    dims = values.shape
    index_at = [jax.random.randint(jax.random.fold_in(own_key, axis), (), 0, dims[axis]) for axis in range(len(dims))]
    values = values.at[tuple(index_at)].set(smallest)
    longest = dims.index(max(dims))
    index_at[longest] = (index_at[longest] + 1) % dims[longest]
    return values.at[tuple(index_at)].set(top_value)


def steps_of(key, extent, pieces, least, top_value):
    def one(position, parts):
        draws = jax.random.uniform(jax.random.fold_in(jax.random.fold_in(key, 6), position), (parts,), jnp.float32, least / len(pieces), top_value / len(pieces))
        return jnp.repeat(jnp.exp(draws), extent[position] // parts).reshape((-1,) + (1,) * (len(extent) - position - 1))

    factor_of = one(*pieces[0])
    for cut in pieces[1:]:
        factor_of = factor_of * one(*cut)
    return factor_of


def noise(stream_key, dims, deviation, bound, cuts=(), kind=jnp.bfloat16):
    values = deviation * jax.random.normal(stream_key, dims, jnp.float32)
    if cuts:
        values = values * steps_of(stream_key, dims, cuts, -0.22, 0.18)
    return jnp.clip(values, -bound, bound).astype(kind)


def setup_inputs(seed: int = 0) -> dict:
    key_of = jax.random.split(jax.random.key(seed), 7)
    return {
        "factor": noise(key_of[0], (POLES, 2, NA, S, W), (NA // 2) ** -0.5, 0.375, ((0, 8), (2, 16)), jnp.float32),
        "green": noise(key_of[1], (POLES, 2, NA, NA), 1.0, 6.0, ((0, 8), (2, 16), (3, 8)), jnp.float32),
        "diag_inv": noise(key_of[2], (POLES, 2, S, W, W), 1.0, 6.0, ((0, 8), (2, 16)), jnp.float32),
        "pole_weight": noise(key_of[3], (POLES, 2), 1.0, 4.0, ((0, 8),), jnp.float32),
        "structure": set_ends((jax.random.randint(key_of[4], (S, NB), 0, 2) < 1).astype(jnp.int32), jax.random.fold_in(key_of[4], 1), 0, 1),
        "widths": draw_widths(jax.random.fold_in(key_of[6], 71), 0),
    }


highest = lax.Precision.HIGHEST


def contract(form, left, right):
    return jnp.einsum(form, left, right, precision=highest, preferred_element_type=jnp.float32)


def offdiag_term(lower_part, green_part):
    real_part = contract("akw,ac->kwc", lower_part[1], green_part[1]) - contract("akw,ac->kwc", lower_part[0], green_part[0])
    imag_part = -(contract("akw,ac->kwc", lower_part[0], green_part[1]) + contract("akw,ac->kwc", lower_part[1], green_part[0]))
    return jnp.stack([real_part, imag_part], axis=1)


def diag_product(row_inv, lower_cols):
    real_part = contract("kwc,ckv->kwv", row_inv[:, 0], lower_cols[0]) - contract("kwc,ckv->kwv", row_inv[:, 1], lower_cols[1])
    imag_part = contract("kwc,ckv->kwv", row_inv[:, 0], lower_cols[1]) + contract("kwc,ckv->kwv", row_inv[:, 1], lower_cols[0])
    return real_part, imag_part


def reference(factor, green, diag_inv, pole_weight, structure, widths):
    mask_rows = jnp.repeat(structure.astype(jnp.float32), NA // NB, axis=1)
    mask_cols = (jnp.arange(W)[None, :] < widths[:, None]).astype(jnp.float32)
    diag_mask = mask_cols[:, :, None] * mask_cols[:, None, :]
    off_mask = mask_cols[:, :, None] * mask_rows[:, None, :]

    def one_pole(carry, items):
        factor_pole, green_pole, inverse_pole, weight_pole = items
        lower_full = factor_pole * mask_rows.T[None, :, :, None] * mask_cols[None, None, :, :]
        row_inv = offdiag_term(lower_full, green_pole)
        real_part, imag_part = diag_product(row_inv, lower_full)
        diag_term = weight_pole[0] * (inverse_pole[1] - imag_part) + weight_pole[1] * (inverse_pole[0] - real_part)
        off_term = weight_pole[0] * row_inv[:, 1] + weight_pole[1] * row_inv[:, 0]
        return (carry[0] + off_term * off_mask, carry[1] + diag_term * diag_mask), None

    initial = (jnp.zeros((S, W, NA), jnp.float32), jnp.zeros((S, W, W), jnp.float32))
    result, ignored = lax.scan(one_pole, initial, (factor, green, diag_inv, pole_weight))
    return (result[0], result[1])
```

```python
import jax
import jax.numpy as jnp
from jax import lax
from jax.experimental import pallas as pl
from jax.experimental.pallas import tpu as pltpu
from jax.sharding import PartitionSpec as P

VMEM = pl.BlockSpec(memory_space=pltpu.VMEM)
SMEM = pl.BlockSpec(memory_space=pltpu.SMEM)


def split(value):
    high = value.astype(jnp.bfloat16)
    return high, (value - high.astype(jnp.float32)).astype(jnp.bfloat16)


def product(left, right):
    left_high, left_low = split(left)
    right_high, right_low = split(right)

    def one(a, b):
        return lax.dot_general(a, b, (((0,), (0,)), ((), ())), preferred_element_type=jnp.float32)

    return one(left_high, right_high) + (one(left_high, right_low) + one(left_low, right_high))


def compute(cols_here, rows_here, block_rows, poles, held, inverse, weight, structure, widths, sent):
    node = lax.axis_index("row")
    col = lax.axis_index("col")
    owners = held.shape[0]
    width = held.shape[2]
    real_weight, imag_weight = weight[0, 0], weight[0, 1]

    def present(block):
        return structure[block, node].astype(jnp.float32)

    green = jnp.concatenate(
        [held[r, 2 * rows_here :, :] * present(r * rows_here // block_rows) for r in range(owners)], axis=0
    )
    lower = jnp.concatenate(
        [
            held[:, :rows_here, :].reshape(owners * rows_here, width),
            held[:, rows_here : 2 * rows_here, :].reshape(owners * rows_here, width),
        ],
        axis=1,
    )
    parts = product(green, lower)
    real_part = parts[cols_here:, width:] - parts[:cols_here, :width]
    imag_part = -(parts[cols_here:, :width] + parts[:cols_here, width:])
    keep_lane = (lax.broadcasted_iota(jnp.int32, (cols_here, width), 1) < widths[node]).astype(jnp.float32)
    here = present(col * cols_here // block_rows)
    off_term = (real_weight * imag_part + imag_weight * real_part) * keep_lane * here
    other = (real_weight * real_part - imag_weight * imag_part) * keep_lane * here
    span = cols_here // rows_here
    rows = held[pl.ds(col * span, span), : 2 * rows_here, :]
    lower_cols = jnp.concatenate(
        [rows[:, :rows_here].reshape(cols_here, width), rows[:, rows_here:].reshape(cols_here, width)], axis=0
    )
    diag = product(jnp.concatenate([off_term, other], axis=0), lower_cols)
    first = (col == 0).astype(jnp.float32)
    keep = (lax.broadcasted_iota(jnp.int32, (width, width), 1) < widths[node]) & (
        lax.broadcasted_iota(jnp.int32, (width, width), 0) < widths[node]
    )
    diag = (first * (real_weight * inverse[1] + imag_weight * inverse[0]) - diag) * keep.astype(jnp.float32)
    diag_rows, off_rows = width // poles, cols_here // poles
    sent[:, :diag_rows, :] = diag.reshape(poles, diag_rows, width)
    sent[:, diag_rows:, :] = off_term.reshape(poles, off_rows, width)


def add_poles(cols, diag_rows, held, diag, off):
    total = jnp.sum(held[...], axis=0)
    for c in range(cols):
        diag[c] = total[:diag_rows]
    off[...] = total[diag_rows:]


def add_cols(poles, diag_rows, held, off, sent):
    total = jnp.sum(held[...], axis=0)
    for p in range(poles):
        sent[p, :diag_rows] = total
        sent[p, diag_rows:] = off[...]


def per_device(factor, green, diag_inv, pole_weight, structure, widths):
    poles, rows, cols = (lax.axis_size(name) for name in ("pole", "row", "col"))
    rows_here, node_count, width = factor.shape[2:]
    cols_here = green.shape[3]
    block_rows = rows_here * rows // structure.shape[1]
    diag_rows, off_rows = width // poles, cols_here // poles
    f32 = jnp.float32

    lower = factor[0].transpose(2, 0, 1, 3).reshape(node_count, 2 * rows_here, width)
    packed = jnp.concatenate([green[0, 0], green[0, 1]], axis=1)
    packed = jnp.broadcast_to(packed[None], (node_count, rows_here, 2 * cols_here))
    held = lax.all_to_all(jnp.concatenate([lower, packed], axis=1), "row", 0, 0, tiled=True)

    sent = pl.pallas_call(
        lambda *refs: compute(cols_here, rows_here, block_rows, poles, *refs),
        out_shape=jax.ShapeDtypeStruct((poles, diag_rows + off_rows, width), f32),
        in_specs=[VMEM, VMEM, SMEM, SMEM, SMEM],
        out_specs=VMEM,
        name="compute",
    )(held, diag_inv[0, :, 0], pole_weight, structure.T, widths)
    held = lax.all_to_all(sent, "pole", 0, 0, tiled=True)
    sent, off = pl.pallas_call(
        lambda *refs: add_poles(cols, diag_rows, *refs),
        out_shape=(
            jax.ShapeDtypeStruct((cols, diag_rows, width), f32),
            jax.ShapeDtypeStruct((off_rows, width), f32),
        ),
        in_specs=[VMEM],
        out_specs=(VMEM, VMEM),
        name="add_poles",
    )(held)
    held = lax.all_to_all(sent, "col", 0, 0, tiled=True)
    sent = pl.pallas_call(
        lambda *refs: add_cols(poles, diag_rows, *refs),
        out_shape=jax.ShapeDtypeStruct((poles, diag_rows + off_rows, width), f32),
        in_specs=[VMEM, VMEM],
        out_specs=VMEM,
        name="add_cols",
    )(held, off)
    held = lax.all_to_all(sent, "pole", 0, 0, tiled=True)
    density_diag = held[:, :diag_rows].reshape(1, width, width)
    density_off = held[:, diag_rows:].reshape(1, cols_here, width).transpose(0, 2, 1)
    return (density_off, density_diag)


def solution(mesh):
    placed = (
        P("pole", None, "row", None, None),
        P("pole", None, "row", "col"),
        P("pole", None, "row", None, None),
        P("pole", None),
        P(),
        P(),
    )
    return jax.shard_map(
        per_device,
        mesh=mesh,
        in_specs=placed,
        out_specs=(P("row", None, "col"), P("row", None, None)),
        check_vma=False,
    )
```

```python
import jax
import jax.numpy as jnp
from jax import lax
from jax.experimental import pallas as pl
from jax.experimental.pallas import tpu as pltpu
from jax.sharding import Mesh, PartitionSpec as P

LIMIT = 8 * 1024 * 1024
PACK_LIMIT = 60 * 1024 * 1024
ANY = pl.BlockSpec(memory_space=pl.ANY)
VMEM = pl.BlockSpec(memory_space=pltpu.VMEM)
SMEM = pl.BlockSpec(memory_space=pltpu.SMEM)
PARAMS = pltpu.CompilerParams(vmem_limit_bytes=LIMIT)


def split(value):
    high = value.astype(jnp.bfloat16)
    return high, (value - high.astype(jnp.float32)).astype(jnp.bfloat16)


def product(left, right):
    left_high, left_low = split(left)
    right_high, right_low = split(right)

    def one(a, b):
        return lax.dot_general(a, b, (((0,), (0,)), ((), ())), preferred_element_type=jnp.float32)

    return one(left_high, right_high) + (one(left_high, right_low) + one(left_low, right_high))


def pack(rows_here, factor, green, weight, structure, widths, sent, scalars, held_green, sems):
    node_here = lax.axis_index("row")
    core = lax.axis_index("core")
    nodes, _, width = sent.shape
    copies = [
        pltpu.make_async_copy(factor.at[0, core, :, node, :], sent.at[node, pl.ds(0, rows_here), :], sems.at[node])
        for node in range(nodes)
    ]
    load = pltpu.make_async_copy(green.at[0], held_green, sems.at[nodes])
    load.start()
    for copy in copies:
        copy.start()
    scalars[0:1, :] = jnp.full((1, width), weight[0, 0])
    scalars[1:2, :] = jnp.full((1, width), weight[0, 1])
    scalars[2:3, :] = jnp.full((1, width), widths[node_here].astype(jnp.float32))
    for block in range(structure.shape[0]):
        scalars[8 + block : 9 + block, :] = jnp.full((1, width), structure[block, node_here].astype(jnp.float32))
    load.wait()
    packed = jnp.concatenate([held_green[0], held_green[1]], axis=1)
    for node in range(nodes):
        sent[node, rows_here:, :] = packed
    for copy in copies:
        copy.wait()


def compute(sizes, mine, other, inverse, scalars, sent):
    cols_here, rows_here, block_rows, poles = sizes
    col = 2 * lax.axis_index("zh") + lax.axis_index("core")
    first_core = lax.axis_index("core") == 0
    owners, _, width = mine.shape
    real_weight, imag_weight, count = scalars[0:1, :], scalars[1:2, :], scalars[2:3, :]

    def part_of(held, start, size):
        return held[pl.ds(start, size), :rows_here, :].reshape(size * rows_here, width)

    def both(start, size, axis):
        one, two = part_of(mine, start, size), part_of(other, start, size)
        return jnp.concatenate([jnp.where(first_core, one, two), jnp.where(first_core, two, one)], axis=axis)

    green = []
    for r in range(owners):
        block = 8 + r * rows_here // block_rows
        green.append(mine[r, rows_here:, :] * scalars[block : block + 1, :])
    parts = product(jnp.concatenate(green, axis=0), both(0, owners, 1))
    real_part = parts[cols_here:, width:] - parts[:cols_here, :width]
    imag_part = -(parts[cols_here:, :width] + parts[:cols_here, width:])

    def keep(rows, axis):
        return (lax.broadcasted_iota(jnp.int32, (rows, width), axis).astype(jnp.float32) < count).astype(jnp.float32)

    keep_lane = keep(cols_here, 1) * scalars[pl.ds(8 + col * cols_here // block_rows, 1), :]
    off_term = (real_weight * imag_part + imag_weight * real_part) * keep_lane
    rest = (real_weight * real_part - imag_weight * imag_part) * keep_lane
    span = cols_here // rows_here
    diag = product(jnp.concatenate([off_term, rest], axis=0), both(col * span, span, 0))
    first = (col == 0).astype(jnp.float32)
    diag = (first * (real_weight * inverse[1] + imag_weight * inverse[0]) - diag) * (keep(width, 1) * keep(width, 0))
    diag_rows, off_rows = width // poles, cols_here // poles
    sent[:, :diag_rows, :] = diag.reshape(poles, diag_rows, width)
    sent[:, diag_rows:, :] = off_term.reshape(poles, off_rows, width)


def add_poles(copies, diag_rows, held, diag, off):
    total = jnp.sum(held[...], axis=0)
    for c in range(copies):
        diag[c] = total[:diag_rows]
    off[...] = total[diag_rows:]


def add_cols(copies, diag_rows, held, off, sent):
    total = jnp.sum(held[...], axis=0)
    for p in range(copies):
        sent[p, :diag_rows] = total
        sent[p, diag_rows:] = off[...]


def deliver(diag_rows, held, diag, off, sems):
    copies = [
        pltpu.make_async_copy(held.at[:, :diag_rows, :], diag, sems.at[0]),
        pltpu.make_async_copy(held.at[:, diag_rows:, :], off, sems.at[1]),
    ]
    for copy in copies:
        copy.start()
    for copy in copies:
        copy.wait()


def per_device(factor, green, diag_inv, pole_weight, structure, widths):
    poles, rows, chips, cores = (lax.axis_size(name) for name in ("pole", "row", "zh", "core"))
    rows_here, node_count, width = factor.shape[2:]
    cols_here = green.shape[3]
    block_rows = rows_here * rows // structure.shape[1]
    diag_rows, off_rows = width // poles, cols_here // poles
    sent_rows = diag_rows + off_rows
    f32 = jnp.float32

    sent, scalars = pl.pallas_call(
        lambda *refs: pack(rows_here, *refs),
        out_shape=(
            jax.ShapeDtypeStruct((node_count, 2 * rows_here, width), f32),
            jax.ShapeDtypeStruct((8 + structure.shape[1], width), f32),
        ),
        in_specs=[ANY, ANY, SMEM, SMEM, SMEM],
        out_specs=(VMEM, VMEM),
        scratch_shapes=[
            pltpu.VMEM((2, rows_here, cols_here), f32),
            pltpu.SemaphoreType.DMA((node_count + 1,)),
        ],
        compiler_params=pltpu.CompilerParams(vmem_limit_bytes=PACK_LIMIT),
        name="pack",
    )(factor, green, pole_weight, structure.T, widths)
    mine = lax.all_to_all(sent, "row", 0, 0, tiled=True)
    other = lax.ppermute(mine, "core", [(0, 1), (1, 0)])
    sent = pl.pallas_call(
        lambda *refs: compute((cols_here, rows_here, block_rows, poles), *refs),
        out_shape=jax.ShapeDtypeStruct((poles, sent_rows, width), f32),
        in_specs=[VMEM, VMEM, VMEM, VMEM],
        out_specs=VMEM,
        compiler_params=PARAMS,
        name="compute",
    )(mine, other, diag_inv[0, :, 0], scalars)
    held = lax.all_to_all(sent, "pole", 0, 0, tiled=True)
    sent, off = pl.pallas_call(
        lambda *refs: add_poles(chips * cores, diag_rows, *refs),
        out_shape=(
            jax.ShapeDtypeStruct((chips * cores, diag_rows, width), f32),
            jax.ShapeDtypeStruct((off_rows, width), f32),
        ),
        in_specs=[VMEM],
        out_specs=(VMEM, VMEM),
        compiler_params=PARAMS,
        name="add_poles",
    )(held)
    held = lax.all_to_all(sent, ("zh", "core"), 0, 0, tiled=True)
    sent = pl.pallas_call(
        lambda *refs: add_cols(poles, diag_rows, *refs),
        out_shape=jax.ShapeDtypeStruct((poles, sent_rows, width), f32),
        in_specs=[VMEM, VMEM],
        out_specs=VMEM,
        compiler_params=PARAMS,
        name="add_cols",
    )(held, off)
    held = lax.all_to_all(sent, "pole", 0, 0, tiled=True)
    diag, off = pl.pallas_call(
        lambda *refs: deliver(diag_rows, *refs),
        out_shape=(
            jax.ShapeDtypeStruct((poles, diag_rows, width), f32),
            jax.ShapeDtypeStruct((poles, off_rows, width), f32),
        ),
        in_specs=[VMEM],
        out_specs=(ANY, ANY),
        scratch_shapes=[pltpu.SemaphoreType.DMA((2,))],
        compiler_params=PARAMS,
        name="deliver",
    )(held)
    density_diag = diag.reshape(1, width, width)
    density_off = off.reshape(1, cols_here, width).transpose(0, 2, 1)
    return (density_off, density_diag)


def solution(mesh):
    poles, rows, cols = (mesh.shape[name] for name in ("pole", "row", "col"))
    finer = Mesh(mesh.devices.reshape(poles, rows, cols // 2, 2), ("pole", "row", "zh", "core"))
    col = ("zh", "core")
    placed = (
        P("pole", None, "row", None, None),
        P("pole", None, "row", col),
        P("pole", None, "row", None, None),
        P("pole", None),
        P(),
        P(),
    )
    return jax.shard_map(
        per_device,
        mesh=finer,
        in_specs=placed,
        out_specs=(P("row", None, col), P("row", None, None)),
        check_vma=False,
    )
```

```python
import jax
import jax.numpy as jnp
from jax import lax
from jax.experimental import pallas as pl
from jax.experimental.pallas import tpu as pltpu
from jax.sharding import Mesh, PartitionSpec as P

LIMIT = 8 * 1024 * 1024
ANY = pl.BlockSpec(memory_space=pl.ANY)
VMEM = pl.BlockSpec(memory_space=pltpu.VMEM)
SMEM = pl.BlockSpec(memory_space=pltpu.SMEM)


def split(value):
    high = value.astype(jnp.bfloat16)
    return high, (value - high.astype(jnp.float32)).astype(jnp.bfloat16)


def product(left, right):
    left_high, left_low = split(left)
    right_high, right_low = split(right)

    def one(a, b):
        return lax.dot_general(a, b, (((0,), (0,)), ((), ())), preferred_element_type=jnp.float32)

    return one(left_high, right_high) + (one(left_high, right_low) + one(left_low, right_high))


def pack(rows_here, factor, green, sent, held_green, sems):
    core = lax.axis_index("core")
    nodes = sent.shape[0]
    load = pltpu.make_async_copy(green.at[0], held_green, sems.at[nodes])
    load.start()
    copies = [
        pltpu.make_async_copy(factor.at[0, core, :, node, :], sent.at[node, pl.ds(0, rows_here), :], sems.at[node])
        for node in range(nodes)
    ]
    for copy in copies:
        copy.start()
    load.wait()
    packed = jnp.concatenate([held_green[0], held_green[1]], axis=1)
    for node in range(nodes):
        sent[node, rows_here:, :] = packed
    for copy in copies:
        copy.wait()


def spell(weight, structure, widths, scalars):
    node_here = lax.axis_index("row")
    width = scalars.shape[1]
    scalars[0:1, :] = jnp.full((1, width), weight[0, 0])
    scalars[1:2, :] = jnp.full((1, width), weight[0, 1])
    scalars[2:3, :] = jnp.full((1, width), widths[node_here].astype(jnp.float32))
    scalars[3:8, :] = jnp.zeros((5, width), jnp.float32)
    for block in range(structure.shape[0]):
        scalars[8 + block : 9 + block, :] = jnp.full((1, width), structure[block, node_here].astype(jnp.float32))


def compute(sizes, mine, other, inverse, scalars, sent):
    cols_here, rows_here, block_rows, poles = sizes
    chip = lax.axis_index("zh")
    first_core = lax.axis_index("core") == 0
    owners, _, width = mine.shape
    real_weight, imag_weight, count = scalars[0:1, :], scalars[1:2, :], scalars[2:3, :]

    def part_of(held, start, size):
        return held[pl.ds(start, size), :rows_here, :].reshape(size * rows_here, width)

    def both(start, size, axis):
        one, two = part_of(mine, start, size), part_of(other, start, size)
        return jnp.concatenate([jnp.where(first_core, one, two), jnp.where(first_core, two, one)], axis=axis)

    def green_of(held):
        rows = []
        for r in range(owners):
            block = 8 + r * rows_here // block_rows
            rows.append(held[r, rows_here:, :] * scalars[block : block + 1, :])
        return jnp.concatenate(rows, axis=0)

    def keep(rows, axis):
        return (lax.broadcasted_iota(jnp.int32, (rows, width), axis).astype(jnp.float32) < count).astype(jnp.float32)

    parts = product(jnp.concatenate([green_of(mine), green_of(other)], axis=1), both(0, owners, 1))
    keep_lane = keep(cols_here, 1)
    span = cols_here // rows_here
    left, right = [], []
    for c in range(2):
        real_rows = parts[2 * c * cols_here : (2 * c + 1) * cols_here]
        imag_rows = parts[(2 * c + 1) * cols_here : (2 * c + 2) * cols_here]
        real_part = imag_rows[:, width:] - real_rows[:, :width]
        imag_part = -(imag_rows[:, :width] + real_rows[:, width:])
        core = lax.axis_index("core")
        col = 2 * chip + (core if c == 0 else 1 - core)
        kept = keep_lane * scalars[pl.ds(8 + col * cols_here // block_rows, 1), :]
        left.append((real_weight * imag_part + imag_weight * real_part) * kept)
        left.append((real_weight * real_part - imag_weight * imag_part) * kept)
        right.append(both(col * span, span, 0))
    diag = product(jnp.concatenate(left, axis=0), jnp.concatenate(right, axis=0))
    first = (chip == 0).astype(jnp.float32)
    diag = (first * (real_weight * inverse[1] + imag_weight * inverse[0]) - diag) * (keep(width, 1) * keep(width, 0))
    diag_rows, off_rows = width // poles, cols_here // poles
    sent[:, :diag_rows, :] = diag.reshape(poles, diag_rows, width)
    sent[:, diag_rows:, :] = left[0].reshape(poles, off_rows, width)


def add_poles(copies, diag_rows, held, diag, off):
    total = jnp.sum(held[...], axis=0)
    for c in range(copies):
        diag[c] = total[:diag_rows]
    off[...] = total[diag_rows:]


def add_cols(copies, diag_rows, held, off, sent):
    total = jnp.sum(held[...], axis=0)
    for p in range(copies):
        sent[p, :diag_rows] = total
        sent[p, diag_rows:] = off[...]


def deliver(diag_rows, held, diag, off, sems):
    copies = [
        pltpu.make_async_copy(held.at[:, :diag_rows, :], diag, sems.at[0]),
        pltpu.make_async_copy(held.at[:, diag_rows:, :], off, sems.at[1]),
    ]
    for copy in copies:
        copy.start()
    for copy in copies:
        copy.wait()


def per_device(factor, green, diag_inv, pole_weight, structure, widths):
    poles, rows, chips = (lax.axis_size(name) for name in ("pole", "row", "zh"))
    rows_here, node_count, width = factor.shape[2:]
    cols_here = green.shape[3]
    block_rows = rows_here * rows // structure.shape[1]
    diag_rows, off_rows = width // poles, cols_here // poles
    sent_rows = diag_rows + off_rows
    f32 = jnp.float32

    def call(body, name, out_shape, in_specs, out_specs, scratch_shapes=()):
        with jax.named_scope(name):
            return pl.pallas_call(
                body,
                out_shape=out_shape,
                in_specs=in_specs,
                out_specs=out_specs,
                scratch_shapes=scratch_shapes,
                compiler_params=pltpu.CompilerParams(vmem_limit_bytes=LIMIT),
                cost_estimate=pl.CostEstimate(flops=1000000, bytes_accessed=1000000, transcendentals=0),
                name=name,
            )

    def shape(*dims):
        return jax.ShapeDtypeStruct(dims, f32)

    def exchange(name, value, axis):
        with jax.named_scope(name):
            return lax.all_to_all(value, axis, 0, 0, tiled=True)

    sent = call(
        lambda *refs: pack(rows_here, *refs),
        "pack",
        shape(node_count, 2 * rows_here, width),
        [ANY, ANY],
        VMEM,
        [
            pltpu.VMEM((2, rows_here, cols_here), f32),
            pltpu.SemaphoreType.DMA((node_count + 1,)),
        ],
    )(pltpu.with_memory_space_constraint(factor, pltpu.HBM), pltpu.with_memory_space_constraint(green, pltpu.HBM))
    scalars = call(spell, "spell", shape(8 + structure.shape[1], width), [SMEM] * 3, VMEM)(
        pole_weight, structure.T, widths
    )
    mine = exchange("over_row", sent, "row")
    with jax.named_scope("swap"):
        other = lax.ppermute(mine, "core", [(0, 1), (1, 0)])
    sent = call(
        lambda *refs: compute((cols_here, rows_here, block_rows, poles), *refs),
        "compute",
        shape(poles, sent_rows, width),
        [VMEM] * 4,
        VMEM,
    )(mine, other, diag_inv[0, :, 0], scalars)
    held = exchange("over_pole", sent, "pole")
    sent, off = call(
        lambda *refs: add_poles(chips, diag_rows, *refs),
        "add_poles",
        (shape(chips, diag_rows, width), shape(off_rows, width)),
        [VMEM],
        (VMEM, VMEM),
    )(held)
    held = exchange("over_chips", sent, "zh")
    sent = call(
        lambda *refs: add_cols(poles, diag_rows, *refs), "add_cols", shape(poles, sent_rows, width), [VMEM, VMEM], VMEM
    )(held, off)
    held = exchange("back_over_pole", sent, "pole")
    diag, off = call(
        lambda *refs: deliver(diag_rows, *refs),
        "deliver",
        (shape(poles, diag_rows, width), shape(poles, off_rows, width)),
        [VMEM],
        (ANY, ANY),
        [pltpu.SemaphoreType.DMA((2,))],
    )(held)
    density_diag = diag.reshape(1, width, width)
    density_off = off.reshape(1, cols_here, width).transpose(0, 2, 1)
    return (density_off, density_diag)


def solution(mesh):
    poles, rows, cols = (mesh.shape[name] for name in ("pole", "row", "col"))
    finer = Mesh(mesh.devices.reshape(poles, rows, cols // 2, 2), ("pole", "row", "zh", "core"))
    col = ("zh", "core")
    placed = (
        P("pole", None, "row", None, None),
        P("pole", None, "row", col),
        P("pole", None, "row", None, None),
        P("pole", None),
        P(),
        P(),
    )
    return jax.shard_map(
        per_device,
        mesh=finer,
        in_specs=placed,
        out_specs=(P("row", None, col), P("row", None, None)),
        check_vma=False,
    )
```
